32 devices in a mesh: spatial: 8 (over z, x), filter: 4 (over y, core).
Axes of the slice: x: 2, y: 2, z: 4, core: 2. Of those that a mesh axis runs over, the one named last changes fastest.
Arguments:
- volume_in: bfloat16 [128, 32, 8192], P('filter', 'spatial'), may hold values from -6 to 6
- filters_a: bfloat16 [27, 256, 128], P(None, 'filter'), may hold values from -0.109375 to 0.109375
- bias_a: bfloat16 [256], P('filter'), may hold values from -0.5 to 0.5
- filters_b: bfloat16 [27, 256, 256], P(None, 'filter'), may hold values from -0.078125 to 0.078125
- bias_b: bfloat16 [256], P('filter'), may hold values from -0.5 to 0.5
Outputs:
- volume_out: bfloat16 [256, 8, 512], P('filter', 'spatial')
The draws below stay inside these ranges and needn't reach their ends.
All inputs are finite; a program needn't handle non-finite values.
Results may differ from the reference program's by a relative error of at most 0.0048.
Values may be sent and summed in bfloat16 or wider, within the bound.
A program may use at most 128 MiB of HBM per device.

```python
import jax
import jax.numpy as jnp
from jax import lax

C_IN = 128
C_MID = 256
ROWS = 64
COLS = 128
DEPTH = 32


def block_levels(rng, extent, shards, least, largest):
    loudness, own = 1.0, jax.random.fold_in(rng, 6)
    for position, shards_of in shards:
        heights = jnp.exp(jax.random.uniform(jax.random.fold_in(own, position), (shards_of,), jnp.float32, least / len(shards), largest / len(shards)))
        loudness = loudness * jnp.repeat(heights, extent[position] // shards_of).reshape([-1 if axis == position else 1 for axis in range(len(extent))])
    return loudness


def gaussian(rng, dims, scale, bound, pieces=(), dtype=jnp.bfloat16):
    array = scale * jax.random.normal(rng, dims, jnp.float32)
    if pieces:
        array = array * block_levels(rng, dims, pieces, -0.22, 0.18)
    return jnp.clip(array, -bound, bound).astype(dtype)


def setup_inputs(seed: int = 0) -> dict:
    key_of = jax.random.split(jax.random.key(seed), 6)
    volume_in = gaussian(key_of[0], (C_IN, DEPTH, ROWS * COLS), 1.0, 6.0, ((0, 4), (1, 8)))
    filters_a = gaussian(key_of[1], (27, C_MID, C_IN), (27 * C_IN) ** -0.5, 0.109375, ((1, 4),))
    bias_a = jnp.clip(jax.random.uniform(key_of[2], (C_MID,), jnp.float32, -0.5, 0.5) * block_levels(key_of[2], (C_MID,), ((0, 4),), -0.4, 0.0), -0.5, 0.5).astype(jnp.bfloat16)
    filters_b = gaussian(key_of[3], (27, C_MID, C_MID), (27 * C_MID) ** -0.5, 0.078125, ((1, 4),))
    bias_b = jnp.clip(jax.random.uniform(key_of[4], (C_MID,), jnp.float32, -0.5, 0.5) * block_levels(key_of[4], (C_MID,), ((0, 4),), -0.4, 0.0), -0.5, 0.5).astype(jnp.bfloat16)
    return dict(volume_in=volume_in, filters_a=filters_a, bias_a=bias_a, filters_b=filters_b, bias_b=bias_b)


def stride_layer(inputs, weight, bias_vec, slices, row_count, col_count):
    channels = inputs.shape[0]
    outputs = weight.shape[1]
    volume = inputs.reshape(1, channels, slices, row_count, col_count)
    kernel = weight.reshape(3, 3, 3, outputs, channels)
    summed = lax.conv_general_dilated(volume, kernel, (2, 2, 2), ((1, 1), (1, 1), (1, 1)), dimension_numbers=("NCDHW", "DHWOI", "NCDHW"), preferred_element_type=jnp.float32)[0]
    summed = summed + bias_vec.astype(jnp.float32)[:, None, None, None]
    active = jnp.where(summed > 0, summed, 0.2 * summed)
    return active.astype(jnp.bfloat16).reshape(outputs, slices // 2, (row_count // 2) * (col_count // 2))


def reference(volume_in, filters_a, bias_a, filters_b, bias_b):
    hidden = stride_layer(volume_in, filters_a, bias_a, DEPTH, ROWS, COLS)
    return stride_layer(hidden, filters_b, bias_b, DEPTH // 2, ROWS // 2, COLS // 2)
```

```python
import jax
import jax.numpy as jnp
import numpy as np
from jax import lax
from jax.experimental import pallas as pl
from jax.experimental.pallas import tpu as pltpu
from jax.sharding import PartitionSpec as P

MESH = pl.DeviceIdType.MESH
ROWS = 64
COLS = 128
F32 = jnp.float32
BF16 = jnp.bfloat16


def shifted(block, axis, distance):
    devices = range(lax.axis_size(axis))
    route = [(i - distance, i) for i in devices if i - distance in devices]
    return lax.ppermute(block, axis, route)


def local_conv(block, weight, pad_rows, row_count, col_count):
    channels = block.shape[0]
    slices = block.shape[1]
    volume = block.reshape(1, channels, slices, row_count, col_count)
    kernel = weight.reshape(3, 3, 3, weight.shape[1], weight.shape[2])
    return lax.conv_general_dilated(
        volume,
        kernel,
        (2, 2, 2),
        ((0, 0), (pad_rows, pad_rows), (1, 1)),
        dimension_numbers=("NCDHW", "DHWOI", "NCDHW"),
        preferred_element_type=F32,
    )[0]


def activate(summed, bias_vec):
    summed = summed + bias_vec.astype(F32)[:, None, None, None]
    return jnp.where(summed > 0, summed, 0.2 * summed).astype(BF16)


def gathered(volume_in, filters_a, bias_a, filters_b, bias_b):
    slices = volume_in.shape[1]
    outputs = filters_a.shape[1]
    extended = jnp.concatenate([shifted(volume_in[:, -1:], "spatial", 1), volume_in], 1)
    full = lax.all_gather(extended, "filter", axis=0, tiled=True)
    hidden = activate(local_conv(full, filters_a, 1, ROWS, COLS), bias_a)
    hidden = hidden.reshape(outputs, slices // 2, ROWS // 2 * (COLS // 2))
    extended = jnp.concatenate([shifted(hidden[:, -1:], "spatial", 1), hidden], 1)
    full = lax.all_gather(extended, "filter", axis=0, tiled=True)
    out = activate(local_conv(full, filters_b, 1, ROWS // 2, COLS // 2), bias_b)
    return out.reshape(filters_b.shape[1], slices // 4, ROWS // 4 * (COLS // 4))


HALF = 2048
QUARTER = 512


def pick_first():
    s = np.zeros((256, 3, 128), np.float32)
    for l in range(3):
        for row in range(2):
            for w in range(64):
                source = 2 * w + l - 1
                if source >= 0:
                    s[row * 128 + source, l, row * 64 + w] = 1
    return s.reshape(256, 384)


def pick_second():
    s = np.zeros((2, 512, 3, 128), np.float32)
    for half in range(2):
        for l in range(3):
            for row in range(4):
                for w in range(32):
                    source = 2 * w + l - 1
                    if source >= 0:
                        s[half, row * 128 + half * 64 + source, l, row * 32 + w] = 1
    return s.reshape(2, 512, 384)


def leaky(u):
    return jnp.where(u > 0, u, 0.2 * u).astype(BF16)


def kernel(
    n_spatial, x, fa, fb, ba, bb, s1, s2, out,
    xh, wa_send, wa, wb_send, wb, v0, v1, part, sib, y_send, y_recv, hid, v2,
    part2, sib2, z_send, z_recv,
    halo_sems, wa_sems, wb_sems, sib_sems, y_sems, hid_sems, sib2_sems, z_sems,
):
    s = lax.axis_index("spatial")
    f = lax.axis_index("filter")
    core, chip = f % 2, f // 2
    sibling = chip * 2 + (1 - core)
    partner = (1 - chip) * 2 + core
    diagonal = (1 - chip) * 2 + (1 - core)
    slot = core * 2 + chip
    peers = (diagonal, partner, sibling)
    is_first, is_last = s == 0, s == n_spatial - 1

    barrier = pltpu.get_barrier_semaphore()
    for peer in peers:
        pl.semaphore_signal(barrier, inc=1, device_id=(s, peer), device_id_type=MESH)

    @pl.when(jnp.logical_not(is_last))
    def _():
        pl.semaphore_signal(barrier, inc=1, device_id=(s + 1, f), device_id_type=MESH)

    @pl.when(jnp.logical_not(is_first))
    def _():
        pl.semaphore_signal(barrier, inc=1, device_id=(s - 1, f), device_id_type=MESH)

    for g in range(4):
        to = (g % 2) * 2 + g // 2
        for b in range(7):
            parts = [fa[t][:, 32 * g : 32 * g + 32] for t in range(4 * b, min(4 * b + 4, 27))]
            if len(parts) < 4:
                parts.append(jnp.zeros((64, 32), BF16))
            wa_send[to, :, 128 * b : 128 * b + 128] = jnp.concatenate(parts, axis=1)

    at_end = jnp.logical_or(is_first, is_last)

    @pl.when(at_end)
    def _():
        pl.semaphore_wait(barrier, 4)

    @pl.when(jnp.logical_not(at_end))
    def _():
        pl.semaphore_wait(barrier, 5)

    def remote(src, dst, sems, target):
        return pltpu.make_async_remote_copy(
            src_ref=src, dst_ref=dst, send_sem=sems[0], recv_sem=sems[1],
            device_id=target, device_id_type=MESH,
        )

    def pair(sems, *index):
        return sems.at[(0,) + index], sems.at[(1,) + index]

    def slot_of(peer):
        return (peer % 2) * 2 + peer // 2

    def weight_copy(send, dst, sems, m):
        return remote(send.at[slot_of(peers[m])], dst.at[slot], pair(sems, m), (s, peers[m]))

    for m in range(3):
        weight_copy(wa_send, wa, wa_sems, m).start()
    halo = remote(x.at[pl.ds(96, 32)], xh, pair(halo_sems), (s + 1, f))

    @pl.when(jnp.logical_not(is_last))
    def _():
        halo.start()

    wa[slot] = wa_send[slot]

    for g in range(4):
        to = (g % 2) * 2 + g // 2
        for b in range(14):
            parts = [fb[t][:, 64 * g : 64 * g + 64] for t in range(2 * b, min(2 * b + 2, 27))]
            if len(parts) < 2:
                parts.append(jnp.zeros((64, 64), BF16))
            wb_send[to, :, 128 * b : 128 * b + 128] = jnp.concatenate(parts, axis=1)
    for m in range(3):
        weight_copy(wb_send, wb, wb_sems, m).start()
    wb[slot] = wb_send[slot]

    def rows_of(ref, t):
        def row(r):
            return ref[:, pl.ds(pl.multiple_of(r * 128, 128), 128)]

        before = jnp.where(t > 0, row(jnp.maximum(4 * t - 1, 0)), jnp.zeros((), BF16))
        one = row(4 * t + 1)
        return (
            jnp.concatenate([before, one], 1),
            jnp.concatenate([row(4 * t), row(4 * t + 2)], 1),
            jnp.concatenate([one, row(4 * t + 3)], 1),
        )

    def taps_own(t, carry):
        cells = jnp.concatenate(rows_of(x, t), 0)
        picked = jnp.dot(cells, s1[...], preferred_element_type=F32).astype(BF16)
        lanes = pl.ds(pl.multiple_of(t * 128, 128), 128)
        for j in range(3):
            for l in range(3):
                for k in range(4):
                    piece = picked[j * 128 + k * 32 : j * 128 + k * 32 + 32, l * 128 : l * 128 + 128]
                    if k > 0:
                        at = ((k - 1) * 9 + 3 * j + l) * 32
                        v1[at : at + 32, lanes] = piece
                    if k < 2:
                        at = ((k + 1) * 9 + 3 * j + l) * 32
                        v0[at : at + 32, lanes] = piece
        return carry

    v0[864:896] = jnp.zeros((32, HALF), BF16)
    v1[864:896] = jnp.zeros((32, HALF), BF16)
    lax.fori_loop(0, 16, taps_own, 0)

    def taps_halo(q, carry):
        cells = jnp.concatenate([c for t in range(4) for c in rows_of(xh, 4 * q + t)], 0)
        picked = jnp.dot(cells, s1[...], preferred_element_type=F32).astype(BF16)
        for t in range(4):
            lanes = pl.ds(pl.multiple_of((4 * q + t) * 128, 128), 128)
            for j in range(3):
                for l in range(3):
                    at = (3 * j + l) * 32
                    row = (3 * t + j) * 32
                    v0[at : at + 32, lanes] = picked[row : row + 32, l * 128 : l * 128 + 128]
        return carry

    def sib_copy(h, u):
        return remote(part.at[h, u, 1 - core], sib.at[h, u], pair(sib_sems, h, u), (s, sibling))

    def y_copy(h, u):
        return remote(y_send.at[h, u], y_recv.at[h, u], pair(y_sems, h, u), (s, partner))

    def first_conv(h, v):
        def body(u, carry):
            lanes = pl.ds(pl.multiple_of(u * 256, 256), 256)
            sums = jnp.dot(wa[...].reshape(256, 896), v[:, lanes], preferred_element_type=F32)
            part[h, u] = sums.reshape(2, 2, 64, 256)
            sib_copy(h, u).start()
            return carry

        lax.fori_loop(0, 8, body, 0)

    def across(h):
        def body(u, carry):
            sib_copy(h, u).wait_recv()
            y_send[h, u] = (part[h, u, core, 1 - chip] + sib[h, u, 1 - chip]).astype(BF16)
            y_copy(h, u).start()
            return carry

        lax.fori_loop(0, 8, body, 0)

    def finish(h, slot_h):
        bias = jnp.broadcast_to(ba[...], (64, 256))

        def body(u, carry):
            y_copy(h, u).wait_recv()
            total = part[h, u, core, chip] + sib[h, u, chip] + y_recv[h, u].astype(F32) + bias
            hid[slot_h, :, pl.ds(pl.multiple_of(u * 256, 256), 256)] = leaky(total)
            return carry

        lax.fori_loop(0, 8, body, 0)

    def second_taps(i):
        def block(q):
            return hid[i, :, 128 * q : 128 * q + 128]

        zero = jnp.zeros((64, 128), BF16)
        now = jnp.concatenate(
            [jnp.concatenate([block(4 * u + r) for r in range(4)], 1) for u in range(4)], 0
        )
        before = jnp.concatenate(
            [
                jnp.concatenate([block(4 * u + r - 1) if 4 * u + r else zero for r in range(4)], 1)
                for u in range(4)
            ],
            0,
        )
        for j, (cells, half) in enumerate(((before, 1), (now, 0), (now, 1))):
            picked = jnp.dot(cells, s2[half], preferred_element_type=F32).astype(BF16)
            for u in range(4):
                for l in range(3):
                    at = (i * 9 + 3 * j + l) * 64
                    v2[at : at + 64, 128 * u : 128 * u + 128] = picked[
                        64 * u : 64 * u + 64, 128 * l : 128 * l + 128
                    ]

    for m in range(3):
        weight_copy(wa_send, wa, wa_sems, m).wait_recv()
    first_conv(1, v1)

    @pl.when(is_first)
    def _():
        xh[...] = jnp.zeros(xh.shape, BF16)

    @pl.when(jnp.logical_not(is_first))
    def _():
        halo.wait_recv()

    across(1)
    lax.fori_loop(0, 4, taps_halo, 0)
    first_conv(0, v0)
    across(0)
    finish(1, 2)
    hid_halo = remote(hid.at[2], hid.at[0], pair(hid_sems), (s + 1, f))

    @pl.when(jnp.logical_not(is_last))
    def _():
        hid_halo.start()

    v2[1728:1792] = jnp.zeros((64, QUARTER), BF16)
    second_taps(2)
    finish(0, 1)
    second_taps(1)

    @pl.when(is_first)
    def _():
        hid[0] = jnp.zeros((64, HALF), BF16)

    @pl.when(jnp.logical_not(is_first))
    def _():
        hid_halo.wait_recv()

    second_taps(0)
    for m in range(3):
        weight_copy(wb_send, wb, wb_sems, m).wait_recv()

    def sib2_copy(u):
        return remote(part2.at[u, 1 - core], sib2.at[u], pair(sib2_sems, u), (s, sibling))

    def z_copy(u):
        return remote(z_send.at[u], z_recv.at[u], pair(z_sems, u), (s, partner))

    for u in range(2):
        lanes = slice(256 * u, 256 * u + 256)
        sums = jnp.dot(wb[...].reshape(256, 1792), v2[:, lanes], preferred_element_type=F32)
        part2[u] = sums.reshape(2, 2, 64, 256)
        sib2_copy(u).start()
    for u in range(2):
        sib2_copy(u).wait_recv()
        z_send[u] = (part2[u, core, 1 - chip] + sib2[u, 1 - chip]).astype(BF16)
        z_copy(u).start()
    bias = jnp.broadcast_to(bb[...], (64, 256))
    for u in range(2):
        z_copy(u).wait_recv()
        total = part2[u, core, chip] + sib2[u, chip] + z_recv[u].astype(F32) + bias
        out[:, 256 * u : 256 * u + 256] = leaky(total)

    for m in range(3):
        weight_copy(wa_send, wa, wa_sems, m).wait_send()
        weight_copy(wb_send, wb, wb_sems, m).wait_send()

    @pl.when(jnp.logical_not(is_last))
    def _():
        halo.wait_send()
        hid_halo.wait_send()

    for h in range(2):

        def drain(u, carry, h=h):
            sib_copy(h, u).wait_send()
            y_copy(h, u).wait_send()
            return carry

        lax.fori_loop(0, 8, drain, 0)
    for u in range(2):
        sib2_copy(u).wait_send()
        z_copy(u).wait_send()


def scattered(n_spatial, volume_in, filters_a, bias_a, filters_b, bias_b):
    x = jnp.transpose(volume_in, (1, 0, 2)).reshape(128, ROWS * COLS)
    vmem = pl.BlockSpec(memory_space=pltpu.VMEM)
    dma = pltpu.SemaphoreType.DMA

    def body(*refs):
        kernel(n_spatial, *refs)

    out = pl.pallas_call(
        body,
        out_shape=jax.ShapeDtypeStruct((64, QUARTER), BF16),
        in_specs=[vmem] * 7,
        out_specs=vmem,
        scratch_shapes=[
            pltpu.VMEM((32, ROWS * COLS), BF16),
            pltpu.VMEM((4, 64, 896), BF16),
            pltpu.VMEM((4, 64, 896), BF16),
            pltpu.VMEM((4, 64, 1792), BF16),
            pltpu.VMEM((4, 64, 1792), BF16),
            pltpu.VMEM((896, HALF), BF16),
            pltpu.VMEM((896, HALF), BF16),
            pltpu.VMEM((2, 8, 2, 2, 64, 256), F32),
            pltpu.VMEM((2, 8, 2, 64, 256), F32),
            pltpu.VMEM((2, 8, 64, 256), BF16),
            pltpu.VMEM((2, 8, 64, 256), BF16),
            pltpu.VMEM((3, 64, HALF), BF16),
            pltpu.VMEM((1792, QUARTER), BF16),
            pltpu.VMEM((2, 2, 2, 64, 256), F32),
            pltpu.VMEM((2, 2, 64, 256), F32),
            pltpu.VMEM((2, 64, 256), BF16),
            pltpu.VMEM((2, 64, 256), BF16),
            dma((2,)), dma((2, 3)), dma((2, 3)), dma((2, 2, 8)), dma((2, 2, 8)), dma((2,)),
            dma((2, 2)), dma((2, 2)),
        ],
        compiler_params=pltpu.CompilerParams(
            collective_id=0, has_side_effects=True, vmem_limit_bytes=52 * 1024 * 1024
        ),
        name="scattered_convs",
    )(
        x,
        filters_a,
        filters_b,
        bias_a.astype(F32).reshape(64, 1),
        bias_b.astype(F32).reshape(64, 1),
        jnp.asarray(pick_first(), BF16),
        jnp.asarray(pick_second(), BF16),
    )
    return out.reshape(64, 1, QUARTER)


def per_device(volume_in, filters_a, bias_a, filters_b, bias_b):
    if volume_in.shape == (32, 4, ROWS * COLS) and filters_b.shape == (27, 64, 256):
        return scattered(lax.axis_size("spatial"), volume_in, filters_a, bias_a, filters_b, bias_b)
    return gathered(volume_in, filters_a, bias_a, filters_b, bias_b)


def solution(mesh):
    in_specs = (
        P("filter", "spatial", None),
        P(None, "filter", None),
        P("filter"),
        P(None, "filter", None),
        P("filter"),
    )
    return jax.shard_map(
        per_device,
        mesh=mesh,
        in_specs=in_specs,
        out_specs=P("filter", "spatial", None),
        check_vma=False,
    )
```

```python
import jax
import jax.numpy as jnp
import numpy as np
from jax import lax
from jax.experimental import pallas as pl
from jax.experimental.pallas import tpu as pltpu
from jax.sharding import PartitionSpec as P

MESH = pl.DeviceIdType.MESH
ROWS = 64
COLS = 128
F32 = jnp.float32
BF16 = jnp.bfloat16


def shifted(block, axis, distance):
    devices = range(lax.axis_size(axis))
    route = [(i - distance, i) for i in devices if i - distance in devices]
    return lax.ppermute(block, axis, route)


def local_conv(block, weight, pad_rows, row_count, col_count):
    channels = block.shape[0]
    slices = block.shape[1]
    volume = block.reshape(1, channels, slices, row_count, col_count)
    kernel = weight.reshape(3, 3, 3, weight.shape[1], weight.shape[2])
    return lax.conv_general_dilated(
        volume,
        kernel,
        (2, 2, 2),
        ((0, 0), (pad_rows, pad_rows), (1, 1)),
        dimension_numbers=("NCDHW", "DHWOI", "NCDHW"),
        preferred_element_type=F32,
    )[0]


def activate(summed, bias_vec):
    summed = summed + bias_vec.astype(F32)[:, None, None, None]
    return jnp.where(summed > 0, summed, 0.2 * summed).astype(BF16)


def gathered(volume_in, filters_a, bias_a, filters_b, bias_b):
    slices = volume_in.shape[1]
    outputs = filters_a.shape[1]
    extended = jnp.concatenate([shifted(volume_in[:, -1:], "spatial", 1), volume_in], 1)
    full = lax.all_gather(extended, "filter", axis=0, tiled=True)
    hidden = activate(local_conv(full, filters_a, 1, ROWS, COLS), bias_a)
    hidden = hidden.reshape(outputs, slices // 2, ROWS // 2 * (COLS // 2))
    extended = jnp.concatenate([shifted(hidden[:, -1:], "spatial", 1), hidden], 1)
    full = lax.all_gather(extended, "filter", axis=0, tiled=True)
    out = activate(local_conv(full, filters_b, 1, ROWS // 2, COLS // 2), bias_b)
    return out.reshape(filters_b.shape[1], slices // 4, ROWS // 4 * (COLS // 4))


HALF = 2048
QUARTER = 512


def pick_first():
    s = np.zeros((256, 3, 128), np.float32)
    for l in range(3):
        for row in range(2):
            for w in range(64):
                source = 2 * w + l - 1
                if source >= 0:
                    s[row * 128 + source, l, row * 64 + w] = 1
    return s.reshape(256, 384)


def pick_second():
    s = np.zeros((2, 512, 3, 128), np.float32)
    for half in range(2):
        for l in range(3):
            for row in range(4):
                for w in range(32):
                    source = 2 * w + l - 1
                    if source >= 0:
                        s[half, row * 128 + half * 64 + source, l, row * 32 + w] = 1
    return s.reshape(2, 512, 384)


def leaky(u):
    return jnp.where(u > 0, u, 0.2 * u).astype(BF16)


def kernel(
    n_spatial, xin, fa, fb_in, ba, bb, s1_in, s2_in, out,
    fb, s1, s2, xv, x, xh, wa_send, wa, wb_send, wb, v0, v1, part, sib, y_send, y_recv, hid, v2,
    part2, sib2, z_send, z_recv,
    in_sems, x_sem, halo_sems, wa_sems, wb_sems, sib_sems, y_sems, hid_sems, sib2_sems, z_sems,
):
    s = lax.axis_index("spatial")
    f = lax.axis_index("filter")
    core, chip = f % 2, f // 2
    sibling = chip * 2 + (1 - core)
    partner = (1 - chip) * 2 + core
    diagonal = (1 - chip) * 2 + (1 - core)
    slot = core * 2 + chip
    peers = (diagonal, partner, sibling)
    is_first, is_last = s == 0, s == n_spatial - 1
    half = (s // 2) % 2
    mate = s + 2 - 4 * half

    load = pltpu.make_async_copy(xin, xv, x_sem)
    load.start()
    load_fb = pltpu.make_async_copy(fb_in, fb, in_sems.at[0])
    load_s1 = pltpu.make_async_copy(s1_in, s1, in_sems.at[1])
    load_s2 = pltpu.make_async_copy(s2_in, s2, in_sems.at[2])
    load_fb.start()
    load_s1.start()
    load_s2.start()
    barrier = pltpu.get_barrier_semaphore()
    for peer in peers:
        pl.semaphore_signal(barrier, inc=1, device_id=(s, peer), device_id_type=MESH)
    pl.semaphore_signal(barrier, inc=1, device_id=(mate, f), device_id_type=MESH)

    @pl.when(jnp.logical_not(is_last))
    def _():
        pl.semaphore_signal(barrier, inc=1, device_id=(s + 1, f), device_id_type=MESH)

    @pl.when(jnp.logical_not(is_first))
    def _():
        pl.semaphore_signal(barrier, inc=1, device_id=(s - 1, f), device_id_type=MESH)

    for g in range(4):
        to = (g % 2) * 2 + g // 2
        for b in range(7):
            parts = [fa[t][:, 32 * g : 32 * g + 32] for t in range(4 * b, min(4 * b + 4, 27))]
            if len(parts) < 4:
                parts.append(jnp.zeros((64, 32), BF16))
            block = jnp.concatenate(parts, axis=1)
            for q in range(2):
                wa_send[to, q, :, 128 * b : 128 * b + 128] = block[32 * q : 32 * q + 32]

    at_end = jnp.logical_or(is_first, is_last)

    @pl.when(at_end)
    def _():
        pl.semaphore_wait(barrier, 5)

    @pl.when(jnp.logical_not(at_end))
    def _():
        pl.semaphore_wait(barrier, 6)

    def remote(src, dst, sems, target):
        return pltpu.make_async_remote_copy(
            src_ref=src, dst_ref=dst, send_sem=sems[0], recv_sem=sems[1],
            device_id=target, device_id_type=MESH,
        )

    def pair(sems, *index):
        return sems.at[(0,) + index], sems.at[(1,) + index]

    def slot_of(peer):
        return (peer % 2) * 2 + peer // 2

    def weight_copy(send, dst, sems, m):
        if m == 2 or send is wa_send or send is wb_send:
            return remote(send.at[slot_of(peers[m])], dst.at[slot], pair(sems, m), (s, peers[m]))
        return remote(
            send.at[slot_of(peers[m]), half], dst.at[slot, half], pair(sems, m), (s, peers[m])
        )

    def forward_copy(dst, sems, m):
        block = dst.at[slot_of(peers[m]), half]
        return remote(block, block, pair(sems, 3 + m), (mate, f))

    def forward(send, dst, sems):
        if send is wa_send or send is wb_send:
            return
        for m in range(2):
            weight_copy(send, dst, sems, m).wait_recv()
            forward_copy(dst, sems, m).start()

    def weights_here(send, dst, sems):
        weight_copy(send, dst, sems, 2).wait_recv()
        for m in range(2):
            if send is wa_send or send is wb_send:
                weight_copy(send, dst, sems, m).wait_recv()
                continue
            forward_copy(dst, sems, m).wait_recv()

    for m in range(3):
        weight_copy(wa_send, wa, wa_sems, m).start()
    wa[slot] = wa_send[slot]

    load_fb.wait()
    for g in range(4):
        to = (g % 2) * 2 + g // 2
        for b in range(14):
            parts = [fb[t][:, 64 * g : 64 * g + 64] for t in range(2 * b, min(2 * b + 2, 27))]
            if len(parts) < 2:
                parts.append(jnp.zeros((64, 64), BF16))
            block = jnp.concatenate(parts, axis=1)
            for q in range(2):
                wb_send[to, q, :, 128 * b : 128 * b + 128] = block[32 * q : 32 * q + 32]
    for m in range(3):
        weight_copy(wb_send, wb, wb_sems, m).start()
    wb[slot] = wb_send[slot]

    load.wait()
    load_s1.wait()

    def by_slice(q, carry):
        lanes = pl.ds(pl.multiple_of(q * 512, 512), 512)
        rows = jnp.swapaxes(xv[:, :, lanes], 0, 1)
        for k in range(4):
            x[32 * k : 32 * k + 32, lanes] = rows[k]
        return carry

    lax.fori_loop(0, 16, by_slice, 0)
    halo = remote(x.at[pl.ds(96, 32)], xh, pair(halo_sems), (s + 1, f))

    @pl.when(jnp.logical_not(is_last))
    def _():
        halo.start()


    def rows_of(ref, t):
        def row(r):
            return ref[:, pl.ds(pl.multiple_of(r * 128, 128), 128)]

        before = jnp.where(t > 0, row(jnp.maximum(4 * t - 1, 0)), jnp.zeros((), BF16))
        one = row(4 * t + 1)
        return (
            jnp.concatenate([before, one], 1),
            jnp.concatenate([row(4 * t), row(4 * t + 2)], 1),
            jnp.concatenate([one, row(4 * t + 3)], 1),
        )

    def taps_own(t, carry):
        cells = jnp.concatenate(rows_of(x, t), 0)
        picked = jnp.dot(cells, s1[...], preferred_element_type=F32).astype(BF16)
        lanes = pl.ds(pl.multiple_of(t * 128, 128), 128)
        for j in range(3):
            for l in range(3):
                for k in range(4):
                    piece = picked[j * 128 + k * 32 : j * 128 + k * 32 + 32, l * 128 : l * 128 + 128]
                    if k > 0:
                        at = ((k - 1) * 9 + 3 * j + l) * 32
                        v1[at : at + 32, lanes] = piece
                    if k < 2:
                        at = ((k + 1) * 9 + 3 * j + l) * 32
                        v0[at : at + 32, lanes] = piece
        return carry

    v0[864:896] = jnp.zeros((32, HALF), BF16)
    v1[864:896] = jnp.zeros((32, HALF), BF16)
    lax.fori_loop(0, 10, taps_own, 0)
    forward(wa_send, wa, wa_sems)
    lax.fori_loop(10, 16, taps_own, 0)

    def taps_halo(q, carry):
        cells = jnp.concatenate([c for t in range(4) for c in rows_of(xh, 4 * q + t)], 0)
        picked = jnp.dot(cells, s1[...], preferred_element_type=F32).astype(BF16)
        for t in range(4):
            lanes = pl.ds(pl.multiple_of((4 * q + t) * 128, 128), 128)
            for j in range(3):
                for l in range(3):
                    at = (3 * j + l) * 32
                    row = (3 * t + j) * 32
                    v0[at : at + 32, lanes] = picked[row : row + 32, l * 128 : l * 128 + 128]
        return carry

    def sib_copy(h, u):
        return remote(part.at[h, u, 1 - core], sib.at[h, u], pair(sib_sems, h, u), (s, sibling))

    def y_copy(h, u):
        return remote(y_send.at[h, u], y_recv.at[h, u], pair(y_sems, h, u), (s, partner))

    def across_one(h, u):
        sib_copy(h, u).wait_recv()
        y_send[h, u] = (part[h, u, core, 1 - chip] + sib[h, u, 1 - chip]).astype(BF16)
        y_copy(h, u).start()

    def across(h):
        across_one(h, 5)
        across_one(h, 6)
        across_one(h, 7)

    def first_conv(h, v):
        def body(u, carry):
            lanes = pl.ds(pl.multiple_of(u * 256, 256), 256)
            sums = jnp.dot(wa[...].reshape(256, 896), v[:, lanes], preferred_element_type=F32)
            part[h, u] = sums.reshape(2, 2, 64, 256)
            sib_copy(h, u).start()

            @pl.when(u >= 3)
            def _():
                across_one(h, u - 3)

            return carry

        lax.fori_loop(0, 8, body, 0)

    def hid_copy(u):
        return remote(hid.at[2, u], hid.at[0, u], pair(hid_sems, u), (s + 1, f))

    def finish(h, slot_h):
        bias = jnp.broadcast_to(ba[...].astype(F32), (64, 256))

        def body(u, carry):
            y_copy(h, u).wait_recv()
            total = part[h, u, core, chip] + sib[h, u, chip] + y_recv[h, u].astype(F32) + bias
            hid[slot_h, u] = leaky(total)
            if slot_h == 2:

                @pl.when(jnp.logical_not(is_last))
                def _():
                    hid_copy(u).start()

            return carry

        lax.fori_loop(0, 8, body, 0)

    def second_taps(i):
        def block(q):
            return hid[i, q // 2, :, 128 * (q % 2) : 128 * (q % 2) + 128]

        zero = jnp.zeros((64, 128), BF16)
        now = jnp.concatenate(
            [jnp.concatenate([block(4 * u + r) for r in range(4)], 1) for u in range(4)], 0
        )
        before = jnp.concatenate(
            [
                jnp.concatenate([block(4 * u + r - 1) if 4 * u + r else zero for r in range(4)], 1)
                for u in range(4)
            ],
            0,
        )
        for j, (cells, half) in enumerate(((before, 1), (now, 0), (now, 1))):
            picked = jnp.dot(cells, s2[half], preferred_element_type=F32).astype(BF16)
            for u in range(4):
                for l in range(3):
                    at = (i * 9 + 3 * j + l) * 64
                    v2[at : at + 64, 128 * u : 128 * u + 128] = picked[
                        64 * u : 64 * u + 64, 128 * l : 128 * l + 128
                    ]

    weights_here(wa_send, wa, wa_sems)
    first_conv(1, v1)
    forward(wb_send, wb, wb_sems)

    @pl.when(is_first)
    def _():
        xh[...] = jnp.zeros(xh.shape, BF16)

    @pl.when(jnp.logical_not(is_first))
    def _():
        halo.wait_recv()

    across(1)
    lax.fori_loop(0, 4, taps_halo, 0)
    first_conv(0, v0)
    across(0)
    finish(1, 2)
    v2[1728:1792] = jnp.zeros((64, QUARTER), BF16)
    load_s2.wait()
    second_taps(2)
    finish(0, 1)
    second_taps(1)

    @pl.when(is_first)
    def _():
        hid[0] = jnp.zeros((8, 64, 256), BF16)

    @pl.when(jnp.logical_not(is_first))
    def _():
        for u in range(8):
            hid_copy(u).wait_recv()

    second_taps(0)
    weights_here(wb_send, wb, wb_sems)

    def sib2_copy(u):
        block = part2.at[u, 1 - core, chip]
        return remote(block, sib2.at[u], pair(sib2_sems, u), (s, sibling))

    def z_copy(u, m):
        return remote(z_send.at[u, m], z_recv.at[u, m], pair(z_sems, u, m), (s, peers[m]))

    for u in range(2):
        lanes = slice(256 * u, 256 * u + 256)
        sums = jnp.dot(wb[...].reshape(256, 1792), v2[:, lanes], preferred_element_type=F32)
        part2[u] = sums.reshape(2, 2, 64, 256)
        for m in range(2):
            to_core = 1 - core if m == 0 else core
            z_send[u, m] = part2[u, to_core, 1 - chip].astype(BF16)
            z_copy(u, m).start()
        sib2_copy(u).start()
    bias = jnp.broadcast_to(bb[...].astype(F32), (64, 256))
    for u in range(2):
        sib2_copy(u).wait_recv()
        for m in range(2):
            z_copy(u, m).wait_recv()
        far = z_recv[u, 0].astype(F32) + z_recv[u, 1].astype(F32)
        total = part2[u, core, chip] + sib2[u] + far + bias
        out[:, 256 * u : 256 * u + 256] = leaky(total)

    for m in range(3):
        weight_copy(wa_send, wa, wa_sems, m).wait_send()
        weight_copy(wb_send, wb, wb_sems, m).wait_send()
    for m in range(2):
        pass
        pass

    @pl.when(jnp.logical_not(is_last))
    def _():
        halo.wait_send()
        for u in range(8):
            hid_copy(u).wait_send()

    for h in range(2):

        def drain(u, carry, h=h):
            sib_copy(h, u).wait_send()
            y_copy(h, u).wait_send()
            return carry

        lax.fori_loop(0, 8, drain, 0)
    for u in range(2):
        sib2_copy(u).wait_send()
        for m in range(2):
            z_copy(u, m).wait_send()


def scattered(n_spatial, volume_in, filters_a, bias_a, filters_b, bias_b):
    vmem = pl.BlockSpec(memory_space=pltpu.VMEM)
    hbm = pl.BlockSpec(memory_space=pl.ANY)
    dma = pltpu.SemaphoreType.DMA

    def body(*refs):
        kernel(n_spatial, *refs)

    out = pl.pallas_call(
        body,
        out_shape=jax.ShapeDtypeStruct((64, QUARTER), BF16),
        in_specs=[hbm, vmem, hbm, vmem, vmem, hbm, hbm],
        out_specs=vmem,
        scratch_shapes=[
            pltpu.VMEM((27, 64, 256), BF16),
            pltpu.VMEM((256, 384), BF16),
            pltpu.VMEM((2, 512, 384), BF16),
            pltpu.VMEM((32, 4, ROWS * COLS), BF16),
            pltpu.VMEM((128, ROWS * COLS), BF16),
            pltpu.VMEM((32, ROWS * COLS), BF16),
            pltpu.VMEM((4, 2, 32, 896), BF16),
            pltpu.VMEM((4, 2, 32, 896), BF16),
            pltpu.VMEM((4, 2, 32, 1792), BF16),
            pltpu.VMEM((4, 2, 32, 1792), BF16),
            pltpu.VMEM((896, HALF), BF16),
            pltpu.VMEM((896, HALF), BF16),
            pltpu.VMEM((2, 8, 2, 2, 64, 256), F32),
            pltpu.VMEM((2, 8, 2, 64, 256), F32),
            pltpu.VMEM((2, 8, 64, 256), BF16),
            pltpu.VMEM((2, 8, 64, 256), BF16),
            pltpu.VMEM((3, 8, 64, 256), BF16),
            pltpu.VMEM((1792, QUARTER), BF16),
            pltpu.VMEM((2, 2, 2, 64, 256), F32),
            pltpu.VMEM((2, 64, 256), F32),
            pltpu.VMEM((2, 2, 64, 256), BF16),
            pltpu.VMEM((2, 2, 64, 256), BF16),
            dma((3,)), dma, dma((2,)), dma((2, 5)), dma((2, 5)), dma((2, 2, 8)), dma((2, 2, 8)), dma((2, 8)),
            dma((2, 2)), dma((2, 2, 2)),
        ],
        compiler_params=pltpu.CompilerParams(
            collective_id=0, has_side_effects=True, vmem_limit_bytes=52 * 1024 * 1024
        ),
        name="scattered_convs",
    )(
        volume_in,
        filters_a,
        filters_b,
        bias_a.reshape(64, 1),
        bias_b.reshape(64, 1),
        jnp.asarray(pick_first(), BF16),
        jnp.asarray(pick_second(), BF16),
    )
    return out.reshape(64, 1, QUARTER)


def per_device(volume_in, filters_a, bias_a, filters_b, bias_b):
    n_spatial = lax.axis_size("spatial")
    own = volume_in.shape == (32, 4, ROWS * COLS) and filters_b.shape == (27, 64, 256)
    if own and n_spatial % 4 == 0:
        return scattered(n_spatial, volume_in, filters_a, bias_a, filters_b, bias_b)
    return gathered(volume_in, filters_a, bias_a, filters_b, bias_b)


def solution(mesh):
    in_specs = (
        P("filter", "spatial", None),
        P(None, "filter", None),
        P("filter"),
        P(None, "filter", None),
        P("filter"),
    )
    return jax.shard_map(
        per_device,
        mesh=mesh,
        in_specs=in_specs,
        out_specs=P("filter", "spatial", None),
        check_vma=False,
    )
```

```python
import jax
import jax.numpy as jnp
import numpy as np
from jax import lax
from jax.experimental import pallas as pl
from jax.experimental.pallas import tpu as pltpu
from jax.sharding import PartitionSpec as P

MESH = pl.DeviceIdType.MESH
ROWS = 64
COLS = 128
F32 = jnp.float32
BF16 = jnp.bfloat16


def shifted(block, axis, distance):
    devices = range(lax.axis_size(axis))
    route = [(i - distance, i) for i in devices if i - distance in devices]
    return lax.ppermute(block, axis, route)


def local_conv(block, weight, pad_rows, row_count, col_count):
    channels = block.shape[0]
    slices = block.shape[1]
    volume = block.reshape(1, channels, slices, row_count, col_count)
    kernel = weight.reshape(3, 3, 3, weight.shape[1], weight.shape[2])
    return lax.conv_general_dilated(
        volume,
        kernel,
        (2, 2, 2),
        ((0, 0), (pad_rows, pad_rows), (1, 1)),
        dimension_numbers=("NCDHW", "DHWOI", "NCDHW"),
        preferred_element_type=F32,
    )[0]


def activate(summed, bias_vec):
    summed = summed + bias_vec.astype(F32)[:, None, None, None]
    return jnp.where(summed > 0, summed, 0.2 * summed).astype(BF16)


def gathered(volume_in, filters_a, bias_a, filters_b, bias_b):
    slices = volume_in.shape[1]
    outputs = filters_a.shape[1]
    extended = jnp.concatenate([shifted(volume_in[:, -1:], "spatial", 1), volume_in], 1)
    full = lax.all_gather(extended, "filter", axis=0, tiled=True)
    hidden = activate(local_conv(full, filters_a, 1, ROWS, COLS), bias_a)
    hidden = hidden.reshape(outputs, slices // 2, ROWS // 2 * (COLS // 2))
    extended = jnp.concatenate([shifted(hidden[:, -1:], "spatial", 1), hidden], 1)
    full = lax.all_gather(extended, "filter", axis=0, tiled=True)
    out = activate(local_conv(full, filters_b, 1, ROWS // 2, COLS // 2), bias_b)
    return out.reshape(filters_b.shape[1], slices // 4, ROWS // 4 * (COLS // 4))


HALF = 2048
QUARTER = 512


def pick_first():
    s = np.zeros((256, 3, 128), np.float32)
    for l in range(3):
        for row in range(2):
            for w in range(64):
                source = 2 * w + l - 1
                if source >= 0:
                    s[row * 128 + source, l, row * 64 + w] = 1
    return s.reshape(256, 384)


def pick_second():
    s = np.zeros((2, 512, 3, 128), np.float32)
    for half in range(2):
        for l in range(3):
            for row in range(4):
                for w in range(32):
                    source = 2 * w + l - 1
                    if source >= 0:
                        s[half, row * 128 + half * 64 + source, l, row * 32 + w] = 1
    return s.reshape(2, 512, 384)


def leaky(u):
    return jnp.where(u > 0, u, 0.2 * u).astype(BF16)


def kernel(
    n_spatial, xin, fa, fb_in, ba, bb, s1_in, s2_in, out,
    fb, s1, s2, xv, x, xh, wa_send, wa, wb_send, wb, v0, v1, part, sib, y_send, y_recv, hid, v2,
    part2, sib2, z_send, z_recv,
    in_sems, x_sem, halo_sems, wa_sems, wb_sems, sib_sems, y_sems, hid_sems, sib2_sems, z_sems,
):
    s = lax.axis_index("spatial")
    f = lax.axis_index("filter")
    core, chip = f % 2, f // 2
    sibling = chip * 2 + (1 - core)
    partner = (1 - chip) * 2 + core
    diagonal = (1 - chip) * 2 + (1 - core)
    slot = core * 2 + chip
    peers = (diagonal, partner, sibling)
    is_first, is_last = s == 0, s == n_spatial - 1
    half = (s // 2) % 2
    mate = s + 2 - 4 * half

    load = pltpu.make_async_copy(xin, xv, x_sem)
    load.start()
    load_fb = pltpu.make_async_copy(fb_in, fb, in_sems.at[0])
    load_s1 = pltpu.make_async_copy(s1_in, s1, in_sems.at[1])
    load_s2 = pltpu.make_async_copy(s2_in, s2, in_sems.at[2])
    load_fb.start()
    load_s1.start()
    load_s2.start()
    barrier = pltpu.get_barrier_semaphore()
    for peer in peers:
        pl.semaphore_signal(barrier, inc=1, device_id=(s, peer), device_id_type=MESH)
    pl.semaphore_signal(barrier, inc=1, device_id=(mate, f), device_id_type=MESH)

    @pl.when(jnp.logical_not(is_last))
    def _():
        pl.semaphore_signal(barrier, inc=1, device_id=(s + 1, f), device_id_type=MESH)

    @pl.when(jnp.logical_not(is_first))
    def _():
        pl.semaphore_signal(barrier, inc=1, device_id=(s - 1, f), device_id_type=MESH)

    for g in range(4):
        to = (g % 2) * 2 + g // 2
        for b in range(7):
            parts = [fa[t][:, 32 * g : 32 * g + 32] for t in range(4 * b, min(4 * b + 4, 27))]
            if len(parts) < 4:
                parts.append(jnp.zeros((64, 32), BF16))
            block = jnp.concatenate(parts, axis=1)
            for q in range(2):
                wa_send[to, q, :, 128 * b : 128 * b + 128] = block[32 * q : 32 * q + 32]

    at_end = jnp.logical_or(is_first, is_last)

    @pl.when(at_end)
    def _():
        pl.semaphore_wait(barrier, 5)

    @pl.when(jnp.logical_not(at_end))
    def _():
        pl.semaphore_wait(barrier, 6)

    def remote(src, dst, sems, target):
        return pltpu.make_async_remote_copy(
            src_ref=src, dst_ref=dst, send_sem=sems[0], recv_sem=sems[1],
            device_id=target, device_id_type=MESH,
        )

    def pair(sems, *index):
        return sems.at[(0,) + index], sems.at[(1,) + index]

    def slot_of(peer):
        return (peer % 2) * 2 + peer // 2

    def weight_copy(send, dst, sems, m):
        if m == 2 or send is wa_send or send is wb_send:
            return remote(send.at[slot_of(peers[m])], dst.at[slot], pair(sems, m), (s, peers[m]))
        return remote(
            send.at[slot_of(peers[m]), half], dst.at[slot, half], pair(sems, m), (s, peers[m])
        )

    def forward_copy(dst, sems, m):
        block = dst.at[slot_of(peers[m]), half]
        return remote(block, block, pair(sems, 3 + m), (mate, f))

    def forward(send, dst, sems):
        if send is wa_send or send is wb_send:
            return
        for m in range(2):
            weight_copy(send, dst, sems, m).wait_recv()
            forward_copy(dst, sems, m).start()

    def weights_here(send, dst, sems):
        weight_copy(send, dst, sems, 2).wait_recv()
        for m in range(2):
            if send is wa_send or send is wb_send:
                weight_copy(send, dst, sems, m).wait_recv()
                continue
            forward_copy(dst, sems, m).wait_recv()

    for m in range(3):
        weight_copy(wa_send, wa, wa_sems, m).start()
    wa[slot] = wa_send[slot]

    load_fb.wait()
    for g in range(4):
        to = (g % 2) * 2 + g // 2
        for b in range(14):
            parts = [fb[t][:, 64 * g : 64 * g + 64] for t in range(2 * b, min(2 * b + 2, 27))]
            if len(parts) < 2:
                parts.append(jnp.zeros((64, 64), BF16))
            block = jnp.concatenate(parts, axis=1)
            for q in range(2):
                wb_send[to, q, :, 128 * b : 128 * b + 128] = block[32 * q : 32 * q + 32]
    for m in range(3):
        weight_copy(wb_send, wb, wb_sems, m).start()
    wb[slot] = wb_send[slot]

    load.wait()
    load_s1.wait()

    def by_slice(q, carry):
        lanes = pl.ds(pl.multiple_of(q * 512, 512), 512)
        rows = jnp.swapaxes(xv[:, :, lanes], 0, 1)
        for k in range(4):
            x[32 * k : 32 * k + 32, lanes] = rows[k]
        return carry

    lax.fori_loop(0, 16, by_slice, 0)
    halo = remote(x.at[pl.ds(96, 32)], xh, pair(halo_sems), (s + 1, f))

    @pl.when(jnp.logical_not(is_last))
    def _():
        halo.start()


    def rows_of(ref, t):
        def row(r):
            return ref[:, pl.ds(pl.multiple_of(r * 128, 128), 128)]

        before = jnp.where(t > 0, row(jnp.maximum(4 * t - 1, 0)), jnp.zeros((), BF16))
        one = row(4 * t + 1)
        return (
            jnp.concatenate([before, one], 1),
            jnp.concatenate([row(4 * t), row(4 * t + 2)], 1),
            jnp.concatenate([one, row(4 * t + 3)], 1),
        )

    def taps_own(t, carry):
        cells = jnp.concatenate(rows_of(x, t), 0)
        picked = jnp.dot(cells, s1[...], preferred_element_type=F32).astype(BF16)
        lanes = pl.ds(pl.multiple_of(t * 128, 128), 128)
        for j in range(3):
            for l in range(3):
                for k in range(4):
                    piece = picked[j * 128 + k * 32 : j * 128 + k * 32 + 32, l * 128 : l * 128 + 128]
                    if k > 0:
                        at = ((k - 1) * 9 + 3 * j + l) * 32
                        v1[at : at + 32, lanes] = piece
                    if k < 2:
                        at = ((k + 1) * 9 + 3 * j + l) * 32
                        v0[at : at + 32, lanes] = piece
        return carry

    v0[864:896] = jnp.zeros((32, HALF), BF16)
    v1[864:896] = jnp.zeros((32, HALF), BF16)
    lax.fori_loop(0, 10, taps_own, 0)
    forward(wa_send, wa, wa_sems)
    lax.fori_loop(10, 16, taps_own, 0)

    def taps_halo(q, carry):
        cells = jnp.concatenate([c for t in range(4) for c in rows_of(xh, 4 * q + t)], 0)
        picked = jnp.dot(cells, s1[...], preferred_element_type=F32).astype(BF16)
        for t in range(4):
            lanes = pl.ds(pl.multiple_of((4 * q + t) * 128, 128), 128)
            for j in range(3):
                for l in range(3):
                    at = (3 * j + l) * 32
                    row = (3 * t + j) * 32
                    v0[at : at + 32, lanes] = picked[row : row + 32, l * 128 : l * 128 + 128]
        return carry

    def sib_copy(h, u):
        return remote(part.at[h, u, 1 - core], sib.at[h, u], pair(sib_sems, h, u), (s, sibling))

    def y_copy(h, u):
        return remote(y_send.at[h, u], y_recv.at[h, u], pair(y_sems, h, u), (s, partner))

    def across_one(h, u):
        sib_copy(h, u).wait_recv()
        y_send[h, u] = (part[h, u, core, 1 - chip] + sib[h, u, 1 - chip]).astype(BF16)
        y_copy(h, u).start()

    def across(h):
        across_one(h, 5)
        across_one(h, 6)
        across_one(h, 7)

    def first_conv(h, v):
        def body(u, carry):
            lanes = pl.ds(pl.multiple_of(u * 256, 256), 256)
            sums = jnp.dot(wa[...].reshape(256, 896), v[:, lanes], preferred_element_type=F32)
            part[h, u] = sums.reshape(2, 2, 64, 256)
            sib_copy(h, u).start()

            @pl.when(u >= 3)
            def _():
                across_one(h, u - 3)

            return carry

        lax.fori_loop(0, 8, body, 0)

    def hid_copy(u):
        return remote(hid.at[2, u], hid.at[0, u], pair(hid_sems, u), (s + 1, f))

    def finish(h, slot_h):
        bias = jnp.broadcast_to(ba[...].astype(F32), (64, 256))

        def body(u, carry):
            y_copy(h, u).wait_recv()
            total = part[h, u, core, chip] + sib[h, u, chip] + y_recv[h, u].astype(F32) + bias
            hid[slot_h, u] = leaky(total)
            if slot_h == 2:

                @pl.when(jnp.logical_not(is_last))
                def _():
                    hid_copy(u).start()

            return carry

        lax.fori_loop(0, 8, body, 0)

    def second_taps(i):
        def block(q):
            return hid[i, q // 2, :, 128 * (q % 2) : 128 * (q % 2) + 128]

        zero = jnp.zeros((64, 128), BF16)
        now = jnp.concatenate(
            [jnp.concatenate([block(4 * u + r) for r in range(4)], 1) for u in range(4)], 0
        )
        before = jnp.concatenate(
            [
                jnp.concatenate([block(4 * u + r - 1) if 4 * u + r else zero for r in range(4)], 1)
                for u in range(4)
            ],
            0,
        )
        for j, (cells, half) in enumerate(((before, 1), (now, 0), (now, 1))):
            picked = jnp.dot(cells, s2[half], preferred_element_type=F32).astype(BF16)
            for u in range(4):
                for l in range(3):
                    at = (i * 9 + 3 * j + l) * 64
                    v2[at : at + 64, 128 * u : 128 * u + 128] = picked[
                        64 * u : 64 * u + 64, 128 * l : 128 * l + 128
                    ]

    weights_here(wa_send, wa, wa_sems)
    first_conv(1, v1)
    forward(wb_send, wb, wb_sems)

    @pl.when(is_first)
    def _():
        xh[...] = jnp.zeros(xh.shape, BF16)

    @pl.when(jnp.logical_not(is_first))
    def _():
        halo.wait_recv()

    across(1)
    lax.fori_loop(0, 4, taps_halo, 0)
    first_conv(0, v0)
    across(0)
    finish(1, 2)
    v2[1728:1792] = jnp.zeros((64, QUARTER), BF16)
    load_s2.wait()
    second_taps(2)
    finish(0, 1)
    second_taps(1)
    weights_here(wb_send, wb, wb_sems)
    for u in range(2):
        lanes = slice(256 * u, 256 * u + 256)
        early = jnp.dot(wb[:, :, :, 640:].reshape(256, 1152), v2[640:, lanes], preferred_element_type=F32)
        part2[u] = early.reshape(2, 2, 64, 256)

    @pl.when(is_first)
    def _():
        hid[0] = jnp.zeros((8, 64, 256), BF16)

    @pl.when(jnp.logical_not(is_first))
    def _():
        for u in range(8):
            hid_copy(u).wait_recv()

    second_taps(0)

    def sib2_copy(u):
        block = part2.at[u, 1 - core, chip]
        return remote(block, sib2.at[u], pair(sib2_sems, u), (s, sibling))

    def z_copy(u, m):
        return remote(z_send.at[u, m], z_recv.at[u, m], pair(z_sems, u, m), (s, peers[m]))

    for u in range(2):
        lanes = slice(256 * u, 256 * u + 256)
        late = jnp.dot(wb[:, :, :, :640].reshape(256, 640), v2[:640, lanes], preferred_element_type=F32)
        part2[u] = part2[u] + late.reshape(2, 2, 64, 256)
        for m in range(2):
            to_core = 1 - core if m == 0 else core
            z_send[u, m] = part2[u, to_core, 1 - chip].astype(BF16)
            z_copy(u, m).start()
        sib2_copy(u).start()
    bias = jnp.broadcast_to(bb[...].astype(F32), (64, 256))
    for u in range(2):
        sib2_copy(u).wait_recv()
        for m in range(2):
            z_copy(u, m).wait_recv()
        far = z_recv[u, 0].astype(F32) + z_recv[u, 1].astype(F32)
        total = part2[u, core, chip] + sib2[u] + far + bias
        out[:, 256 * u : 256 * u + 256] = leaky(total)

    for m in range(3):
        weight_copy(wa_send, wa, wa_sems, m).wait_send()
        weight_copy(wb_send, wb, wb_sems, m).wait_send()
    for m in range(2):
        pass
        pass

    @pl.when(jnp.logical_not(is_last))
    def _():
        halo.wait_send()
        for u in range(8):
            hid_copy(u).wait_send()

    for h in range(2):

        def drain(u, carry, h=h):
            sib_copy(h, u).wait_send()
            y_copy(h, u).wait_send()
            return carry

        lax.fori_loop(0, 8, drain, 0)
    for u in range(2):
        sib2_copy(u).wait_send()
        for m in range(2):
            z_copy(u, m).wait_send()


def scattered(n_spatial, volume_in, filters_a, bias_a, filters_b, bias_b):
    vmem = pl.BlockSpec(memory_space=pltpu.VMEM)
    hbm = pl.BlockSpec(memory_space=pl.ANY)
    dma = pltpu.SemaphoreType.DMA

    def body(*refs):
        kernel(n_spatial, *refs)

    out = pl.pallas_call(
        body,
        out_shape=jax.ShapeDtypeStruct((64, QUARTER), BF16),
        in_specs=[hbm, vmem, hbm, vmem, vmem, hbm, hbm],
        out_specs=vmem,
        scratch_shapes=[
            pltpu.VMEM((27, 64, 256), BF16),
            pltpu.VMEM((256, 384), BF16),
            pltpu.VMEM((2, 512, 384), BF16),
            pltpu.VMEM((32, 4, ROWS * COLS), BF16),
            pltpu.VMEM((128, ROWS * COLS), BF16),
            pltpu.VMEM((32, ROWS * COLS), BF16),
            pltpu.VMEM((4, 2, 32, 896), BF16),
            pltpu.VMEM((4, 2, 32, 896), BF16),
            pltpu.VMEM((4, 2, 32, 1792), BF16),
            pltpu.VMEM((4, 2, 32, 1792), BF16),
            pltpu.VMEM((896, HALF), BF16),
            pltpu.VMEM((896, HALF), BF16),
            pltpu.VMEM((2, 8, 2, 2, 64, 256), F32),
            pltpu.VMEM((2, 8, 2, 64, 256), F32),
            pltpu.VMEM((2, 8, 64, 256), BF16),
            pltpu.VMEM((2, 8, 64, 256), BF16),
            pltpu.VMEM((3, 8, 64, 256), BF16),
            pltpu.VMEM((1792, QUARTER), BF16),
            pltpu.VMEM((2, 2, 2, 64, 256), F32),
            pltpu.VMEM((2, 64, 256), F32),
            pltpu.VMEM((2, 2, 64, 256), BF16),
            pltpu.VMEM((2, 2, 64, 256), BF16),
            dma((3,)), dma, dma((2,)), dma((2, 5)), dma((2, 5)), dma((2, 2, 8)), dma((2, 2, 8)), dma((2, 8)),
            dma((2, 2)), dma((2, 2, 2)),
        ],
        compiler_params=pltpu.CompilerParams(
            collective_id=0, has_side_effects=True, vmem_limit_bytes=52 * 1024 * 1024
        ),
        name="scattered_convs",
    )(
        volume_in,
        filters_a,
        filters_b,
        bias_a.reshape(64, 1),
        bias_b.reshape(64, 1),
        jnp.asarray(pick_first(), BF16),
        jnp.asarray(pick_second(), BF16),
    )
    return out.reshape(64, 1, QUARTER)


def per_device(volume_in, filters_a, bias_a, filters_b, bias_b):
    n_spatial = lax.axis_size("spatial")
    own = volume_in.shape == (32, 4, ROWS * COLS) and filters_b.shape == (27, 64, 256)
    if own and n_spatial % 4 == 0:
        return scattered(n_spatial, volume_in, filters_a, bias_a, filters_b, bias_b)
    return gathered(volume_in, filters_a, bias_a, filters_b, bias_b)


def solution(mesh):
    in_specs = (
        P("filter", "spatial", None),
        P(None, "filter", None),
        P("filter"),
        P(None, "filter", None),
        P("filter"),
    )
    return jax.shard_map(
        per_device,
        mesh=mesh,
        in_specs=in_specs,
        out_specs=P("filter", "spatial", None),
        check_vma=False,
    )
```
